32 devices in a mesh: seq: 8 (over z, core), fsdp: 4 (over y, x).
Axes of the slice: x: 2, y: 2, z: 4, core: 2. Of those that a mesh axis runs over, the one named last changes fastest.
Arguments:
- hidden: bfloat16 [4, 2048, 3584], P('fsdp', 'seq'), may hold values from -6 to 6
- queries: bfloat16 [4, 2048, 2048], P('fsdp', 'seq'), may hold values from -6 to 6
- norm_gain: float32 [3584], replicated, may hold values from 0.1 to 1.9
- key_weight: bfloat16 [3584, 1024], P('fsdp'), may hold values from -0.09375 to 0.09375
- value_weight: bfloat16 [3584, 1024], P('fsdp'), may hold values from -0.09375 to 0.09375
- lengths: int32 [4], P('fsdp'), may hold values from 128 to 2048, as said below
Outputs:
- attended: bfloat16 [4, 2048, 2048], P('fsdp', 'seq')
The draws below stay inside these ranges and needn't reach their ends.
Inputs may be any that keep to these rules, and one draw needn't show every extreme that they name: `lengths`: each length is a multiple of 128; in every draw some request fills all 2048 slots.
All inputs are finite; a program needn't handle non-finite values.
Results may differ from the reference program's by a relative error of at most 0.0082.
Values may be sent and summed in bfloat16 or wider, within the bound.
No kernel may reach another device: no remote copies, remote signals or barrier semaphores. Data moves between devices by JAX's collectives and lax.ppermute only.
A program may use at most 128 MiB of HBM per device.

```python
import jax
import jax.numpy as jnp
from jax import lax

D = 3584
HQ = 8
HK = 4
HD = 256
WINDOW = 4096
GRAIN = 128
TOK_DEV = 256
REQUESTS = 4
LENGTH = 2048


def draw_lengths(key, part):
    blocks = jax.random.randint(key, (REQUESTS,), 1, LENGTH // GRAIN + 1)
    chosen = jax.random.randint(jax.random.fold_in(key, 7), (), 0, REQUESTS)
    filled = jnp.where(jnp.arange(REQUESTS) == chosen, LENGTH // GRAIN, blocks)
    return (filled * GRAIN).astype(jnp.int32)


def steps_of(key, shape, pieces, least, largest):
    def one(axis_at, shards_of):
        steps = jax.random.uniform(jax.random.fold_in(jax.random.fold_in(key, 6), axis_at), (shards_of,), jnp.float32, least / len(pieces), largest / len(pieces))
        return jnp.repeat(jnp.exp(steps), shape[axis_at] // shards_of).reshape((-1,) + (1,) * (len(shape) - axis_at - 1))

    gain = one(*pieces[0])
    for cut in pieces[1:]:
        gain = gain * one(*cut)
    return gain


def normal_values(rng, shape, width, bound, pieces=(), kind=jnp.bfloat16):
    drawn = jax.random.normal(rng, shape, jnp.float32) * width
    if len(pieces) > 0:
        drawn = steps_of(rng, shape, pieces, -0.22, 0.18) * drawn
    return jnp.clip(drawn, min=-bound, max=bound).astype(kind)


def setup_inputs(seed: int = 0) -> dict:
    key_of = jax.random.split(jax.random.key(seed), 7)
    hidden = normal_values(key_of[0], (REQUESTS, LENGTH, D), 1.0, 6.0, ((0, 4), (1, 8)))
    queries = normal_values(key_of[1], (REQUESTS, LENGTH, HQ * HD), 1.0, 6.0, ((0, 4), (1, 8)))
    norm_gain = jnp.clip(1.0 + 0.18 * jax.random.normal(key_of[2], (D,), jnp.float32), 0.1, 1.9)
    key_weight = normal_values(key_of[3], (D, HK * HD), D ** -0.5, 0.09375, ((0, 4),))
    value_weight = normal_values(key_of[4], (D, HK * HD), D ** -0.5, 0.09375, ((0, 4),))
    lengths = draw_lengths(jax.random.fold_in(key_of[6], 71), 0)
    return {"hidden": hidden, "queries": queries, "norm_gain": norm_gain, "key_weight": key_weight, "value_weight": value_weight, "lengths": lengths}


EPSILON = 1e-06
SOFTCAP = 50.0

def rotate(vectors, positions):
    halfway = vectors.shape[-1] // 2
    exponent = jnp.arange(halfway, dtype=jnp.float32) * (2.0 / vectors.shape[-1])
    frequency = jnp.exp(-jnp.log(10000.0) * exponent)
    angles = positions[:, None] * frequency[None, :]
    cosine = jnp.cos(angles)[:, None, :]
    sine = jnp.sin(angles)[:, None, :]
    first_half = vectors[..., :halfway]
    second_half = vectors[..., halfway:]
    return jnp.concatenate([first_half * cosine - second_half * sine, second_half * cosine + first_half * sine], axis=-1)

def normalize(activations, norm_gain):
    floats = activations.astype(jnp.float32)
    factor = lax.rsqrt(lax.optimization_barrier(jnp.mean(floats * floats, axis=-1, keepdims=True)) + EPSILON)
    return (floats * factor * norm_gain.astype(jnp.float32)).astype(jnp.bfloat16)

def attend(query_rows, key_rows, value_rows, query_pos, key_pos, length):
    scores = jnp.einsum('qgjd,kgd->gjqk', query_rows.astype(jnp.float32), key_rows.astype(jnp.float32))
    scores = scores * (1.0 / jnp.sqrt(jnp.float32(query_rows.shape[-1])))
    capped = SOFTCAP * jnp.tanh(scores / SOFTCAP)
    visible = (key_pos[None, :] <= query_pos[:, None]) & (query_pos[:, None] - key_pos[None, :] < WINDOW)
    visible = visible & (key_pos[None, :] < length) & (key_pos[None, :] >= 0)
    weights = jnp.where(visible[None, None], jnp.exp(capped), 0.0)
    denominator = lax.optimization_barrier(jnp.sum(weights, axis=-1))
    rounded = weights.astype(jnp.bfloat16).astype(jnp.float32)
    numerator = jnp.einsum('gjqk,kgd->qgjd', rounded, value_rows.astype(jnp.float32))
    valid = query_pos < length
    safe_total = jnp.where(valid[None, None, :], denominator, 1.0)
    result = numerator / jnp.transpose(safe_total, (2, 0, 1))[..., None]
    return jnp.where(valid[:, None, None, None], result, 0.0).astype(jnp.bfloat16)

def one_request(hidden_row, query_row, length, norm_gain, key_weight, value_weight):
    normed = normalize(hidden_row, norm_gain)
    positions = jnp.arange(LENGTH, dtype=jnp.int32).astype(jnp.float32)
    key_proj = jnp.dot(normed, key_weight, preferred_element_type=jnp.float32)
    value_proj = jnp.dot(normed, value_weight, preferred_element_type=jnp.float32)
    key_heads = rotate(key_proj.reshape(LENGTH, HK, HD), positions).astype(jnp.bfloat16)
    value_heads = value_proj.astype(jnp.bfloat16).reshape(LENGTH, HK, HD)
    query_heads = rotate(query_row.astype(jnp.float32).reshape(LENGTH, HQ, HD), positions)
    query_heads = query_heads.astype(jnp.bfloat16).reshape(LENGTH, HK, HQ // HK, HD)
    margin = (WINDOW + TOK_DEV - 1) // TOK_DEV * TOK_DEV
    key_padded = jnp.concatenate([jnp.zeros((margin, HK, HD), jnp.bfloat16), key_heads], axis=0)
    value_padded = jnp.concatenate([jnp.zeros((margin, HK, HD), jnp.bfloat16), value_heads], axis=0)

    def block(block_index):
        first = block_index * TOK_DEV
        query_rows = lax.dynamic_slice_in_dim(query_heads, first, TOK_DEV, 0)
        key_rows = lax.dynamic_slice_in_dim(key_padded, first, margin + TOK_DEV, 0)
        value_rows = lax.dynamic_slice_in_dim(value_padded, first, margin + TOK_DEV, 0)
        query_pos = first + jnp.arange(TOK_DEV, dtype=jnp.int32)
        key_pos = first - margin + jnp.arange(margin + TOK_DEV, dtype=jnp.int32)
        return attend(query_rows, key_rows, value_rows, query_pos, key_pos, length)
    blocks = lax.map(block, jnp.arange(LENGTH // TOK_DEV, dtype=jnp.int32))
    return blocks.reshape(LENGTH, HQ * HD)

def reference(hidden, queries, norm_gain, key_weight, value_weight, lengths):

    def per_request(items):
        return one_request(items[0], items[1], items[2], norm_gain, key_weight, value_weight)
    return lax.map(per_request, (hidden, queries, lengths))
```

```python
import functools
import math

import jax
import jax.numpy as jnp
from jax import lax
from jax.experimental import pallas as pl
from jax.experimental.pallas import tpu as pltpu
from jax.sharding import PartitionSpec as P

HQ = 8
HK = 4
HD = 256
WINDOW = 4096

EPSILON = 1e-06
SOFTCAP = 50.0
CORES = 2
HEADS = HK // CORES
GROUP = HQ // HK
MIB = 1 << 20


VMEM = pl.BlockSpec(memory_space=pltpu.VMEM)
SMEM = pl.BlockSpec(memory_space=pltpu.SMEM)


def prep_kernel(meta, own, other, gain, q_own, q_other, cosine, sine, normed, rotated):
    core = meta[0]
    rows = own.shape[0]
    groups, _, depth = normed.shape
    for ref, q_ref, place in ((own, q_own, core), (other, q_other, 1 - core)):
        first = pl.multiple_of(place * rows, rows)
        floats = ref[...].astype(jnp.float32)
        factor = lax.rsqrt(jnp.mean(floats * floats, axis=-1, keepdims=True) + EPSILON)
        result = (floats * factor * gain[...]).astype(jnp.bfloat16)
        for g in range(groups):
            normed[g, pl.ds(first, rows), :] = result[:, g * depth : (g + 1) * depth]
        cos = cosine[pl.ds(first, rows), :]
        sin = sine[pl.ds(first, rows), :]
        scale = 1.0 / (math.sqrt(HD) * SOFTCAP)
        for h in range(rotated.shape[0]):
            a = q_ref[:, h * HD : h * HD + HD // 2].astype(jnp.float32)
            b = q_ref[:, h * HD + HD // 2 : (h + 1) * HD].astype(jnp.float32)
            turned = jnp.concatenate([a * cos - b * sin, b * cos + a * sin], axis=-1)
            rotated[h, pl.ds(first, rows), :] = (turned * scale).astype(jnp.bfloat16)


def project_kernel(rope, meta, normed, cosine, sine, *refs):
    pieces, out = refs[:-1], refs[-1]
    total = None
    for i, piece in enumerate(pieces):
        term = jnp.dot(normed[meta[3 + i]], piece[...], preferred_element_type=jnp.float32)
        total = term if total is None else total + term
    if rope:
        a, b = total[:, : HD // 2], total[:, HD // 2 :]
        cos, sin = cosine[...], sine[...]
        total = jnp.concatenate([a * cos - b * sin, b * cos + a * sin], axis=-1)
    out[...] = total.astype(jnp.bfloat16)


def weigh(query, key, mask):
    scores = lax.dot_general(query, key, (((1,), (1,)), ((), ())), preferred_element_type=jnp.float32)
    weights = jnp.exp2(jnp.tanh(scores) * (SOFTCAP * math.log2(math.e)))
    if mask is not None:
        weights = jnp.where(mask, weights, 0.0)
    return weights


def attend_kernel(window, meta, rotated, *refs):
    count = (len(refs) - 4) // 2
    keys, values = refs[:count], refs[count : 2 * count]
    out_own, out_other, total, mixture = refs[2 * count :]
    core, chip, length = meta[0], meta[1], meta[2]
    heads, rows, _ = rotated.shape
    first = chip * rows

    def visible(query_from, key_from, shape):
        q = query_from + lax.broadcasted_iota(jnp.int32, shape, 0)
        k = key_from + lax.broadcasted_iota(jnp.int32, shape, 1)
        mask = (k <= q) & (k < length)
        if window is not None:
            mask = mask & (q - k < window)
        return mask

    half = rows // CORES
    for part in range(CORES):
        lo, seen = part * half, (part + 1) * half
        mask = visible(first + lo, first, (half, seen))
        for h in range(heads):
            weights = weigh(rotated[h, lo:seen, :], keys[0][:seen, :], mask)
            total[h, lo:seen, :] = jnp.sum(weights, axis=-1, keepdims=True)
            mixture[h, lo:seen, :] = jnp.dot(
                weights.astype(jnp.bfloat16), values[0][:seen, :], preferred_element_type=jnp.float32
            )

    def earlier(step, masked):
        mask = visible(first, first - step * rows, (rows, rows)) if masked else None
        for h in range(heads):
            weights = weigh(rotated[h], keys[step][...], mask)
            total[h] += jnp.sum(weights, axis=-1, keepdims=True)
            mixture[h] += jnp.dot(
                weights.astype(jnp.bfloat16), values[step][...], preferred_element_type=jnp.float32
            )

    for step in range(1, count):
        inside = first - step * rows + rows <= length
        if window is not None:
            inside = inside & ((step + 1) * rows <= window)
        pl.when((chip >= step) & inside)(functools.partial(earlier, step, False))
        pl.when((chip >= step) & jnp.logical_not(inside))(functools.partial(earlier, step, True))

    for ref, place in ((out_own, core), (out_other, 1 - core)):
        at = pl.multiple_of(place * half, half)
        position = first + at + lax.broadcasted_iota(jnp.int32, (half, 1), 0)
        valid = position < length
        for h in range(heads):
            safe = jnp.where(valid, total[h, pl.ds(at, half), :], 1.0)
            result = mixture[h, pl.ds(at, half), :] / safe
            ref[:, h * HD : (h + 1) * HD] = jnp.where(valid, result, 0.0).astype(jnp.bfloat16)


def call(kernel, outs, operands, scratch=(), flops=0, transcendentals=0, limit=None):
    return pl.pallas_call(
        kernel,
        out_shape=outs,
        in_specs=[SMEM] + [VMEM] * (len(operands) - 1),
        out_specs=jax.tree.map(lambda _: VMEM, outs),
        scratch_shapes=list(scratch),
        cost_estimate=pl.CostEstimate(
            flops=flops,
            transcendentals=transcendentals,
            bytes_accessed=sum(x.size * x.dtype.itemsize for x in operands),
        ),
        compiler_params=pltpu.CompilerParams(vmem_limit_bytes=limit),
    )(*operands)


def local(seq, fsdp, hidden, queries, norm_gain, key_weight, value_weight, lengths):
    bf16 = jnp.bfloat16
    _, rows, depth = hidden.shape
    chips = seq // CORES
    block = rows * CORES
    shard = lax.axis_index("seq")
    core, chip = shard % CORES, shard // CORES
    member = lax.axis_index("fsdp")
    relay = fsdp == 4

    swap = [(i, i ^ 1) for i in range(seq)]
    both = ("seq", "fsdp")

    def route(offsets):
        return [
            (i * fsdp + j, i * fsdp + (j ^ offsets[i % CORES]))
            for i in range(seq)
            for j in range(fsdp)
        ]

    def own_heads(x, which):
        return lax.dynamic_slice_in_dim(x, which * (x.shape[1] // CORES), x.shape[1] // CORES, 1)

    order = [(key_weight, 0), (value_weight, 0), (key_weight, 1), (value_weight, 1)]
    pieces = []
    for weight, j in order:
        own = lax.dynamic_slice_in_dim(weight, (core * HEADS + j) * HD, HD, 1)
        if relay:
            near = lax.ppermute(own, both, route((1, 2)))
            next_ = lax.ppermute(own, both, route((2, 1)))
            far = lax.ppermute(near, both, route((2, 1)))
            pieces.append((own, near, next_, far))
        else:
            pieces.append((lax.all_gather(own, "fsdp", axis=0, tiled=True),))
    if relay:
        groups = 4
        ids = [member, member ^ (1 + core), member ^ (2 - core), member ^ 3]
    else:
        groups = 1
        ids = [0]
    meta = jnp.stack([jnp.asarray(v, jnp.int32) for v in [core, chip, lengths[0]] + ids])

    other = lax.ppermute(hidden[0], "seq", swap)
    q_own = own_heads(queries[0], core)
    q_other = lax.ppermute(own_heads(queries[0], 1 - core), "seq", swap)

    exponent = jnp.arange(HD // 2, dtype=jnp.float32) * (2.0 / HD)
    frequency = jnp.exp(-jnp.log(10000.0) * exponent)
    positions = (chip * block + jnp.arange(block, dtype=jnp.int32)).astype(jnp.float32)
    angles = positions[:, None] * frequency[None, :]
    cosine, sine = jnp.cos(angles), jnp.sin(angles)

    normed, rotated = call(
        prep_kernel,
        (
            jax.ShapeDtypeStruct((groups, block, depth // groups), bf16),
            jax.ShapeDtypeStruct((HEADS * GROUP, block, HD), bf16),
        ),
        (meta, hidden[0], other, norm_gain[None, :], q_own, q_other, cosine, sine),
        flops=10 * block * depth,
        limit=40 * MIB,
    )

    climbed = []
    for index, (weight, j) in enumerate(order):
        rope = index % 2 == 0
        made = call(
            functools.partial(project_kernel, rope),
            jax.ShapeDtypeStruct((block, HD), bf16),
            (meta, normed, cosine, sine) + pieces[index],
            flops=2 * block * depth * HD,
            limit=20 * MIB,
        )
        steps = [made]
        for step in range(1, chips):
            pairs = [(i, i + CORES) for i in range((step - 1) * CORES, seq - CORES)]
            steps.append(lax.ppermute(steps[-1], "seq", pairs))
        climbed.append(steps)

    window = WINDOW if WINDOW < chips * block else None
    parts = []
    for j in range(HEADS):
        out_own, out_other = call(
            functools.partial(attend_kernel, window),
            (jax.ShapeDtypeStruct((rows, GROUP * HD), bf16),) * 2,
            (meta, rotated[j * GROUP : (j + 1) * GROUP], *climbed[2 * j], *climbed[2 * j + 1]),
            scratch=(
                pltpu.VMEM((GROUP, block, 1), jnp.float32),
                pltpu.VMEM((GROUP, block, HD), jnp.float32),
            ),
            flops=4 * GROUP * block * block * chips * HD,
            transcendentals=2 * GROUP * block * block * chips,
            limit=24 * MIB,
        )
        parts.append((out_own, lax.ppermute(out_other, "seq", swap)))
    mine = [p[0] for p in parts]
    theirs = [p[1] for p in parts]
    low = [jnp.where(core == 0, a, b) for a, b in zip(mine, theirs)]
    high = [jnp.where(core == 0, b, a) for a, b in zip(mine, theirs)]
    return jnp.concatenate(low + high, axis=1)[None]


def solution(mesh):
    in_specs = (
        P("fsdp", "seq", None),
        P("fsdp", "seq", None),
        P(),
        P("fsdp", None),
        P("fsdp", None),
        P("fsdp"),
    )
    out_specs = P("fsdp", "seq", None)
    body = functools.partial(local, mesh.shape["seq"], mesh.shape["fsdp"])
    return jax.shard_map(body, mesh=mesh, in_specs=in_specs, out_specs=out_specs, check_vma=False)
```

```python
import functools
import math

import jax
import jax.numpy as jnp
from jax import lax
from jax.experimental import pallas as pl
from jax.experimental.pallas import tpu as pltpu
from jax.sharding import PartitionSpec as P


HQ = 8
HK = 4
HD = 256
WINDOW = 4096

EPSILON = 1e-06
SOFTCAP = 50.0
CORES = 2
HEADS = HK // CORES
GROUP = HQ // HK
MIB = 1 << 20


VMEM = pl.BlockSpec(memory_space=pltpu.VMEM)
SMEM = pl.BlockSpec(memory_space=pltpu.SMEM)

KEY, VALUE = "key", "value"
CHUNKS = (
    (KEY, 0, HD, False),
    (VALUE, 0, HD, True),
    (KEY, HD, HD, True),
    (VALUE, HD, HD, True),
)
SPLIT = (1,)


def turn(x, cos, sin):
    a, b = x[:, : HD // 2], x[:, HD // 2 :]
    return jnp.concatenate([a * cos - b * sin, b * cos + a * sin], axis=-1)


def norm_kernel(hidden, gain, normed, lead):
    groups, rows, depth = normed.shape
    floats = hidden[...].astype(jnp.float32)
    factor = lax.rsqrt(jnp.mean(floats * floats, axis=-1, keepdims=True) + EPSILON)
    result = (floats * factor * gain[...]).astype(jnp.bfloat16)
    for g in range(groups):
        normed[g] = result[:, g * depth : (g + 1) * depth]
        lead[g] = result[: rows // 2, g * depth : (g + 1) * depth]


def rope_kernel(meta, q_own, q_other, cosine, sine, rotated):
    core = meta[0]
    rows = q_own.shape[0]
    scale = 1.0 / (math.sqrt(HD) * SOFTCAP)
    for ref, place in ((q_own, core), (q_other, 1 - core)):
        first = pl.multiple_of(place * rows, rows)
        near = pl.multiple_of(place * (rows // 2), rows // 2)
        away = pl.multiple_of(rows + place * (rows // 2), rows // 2)
        cos, sin = (
            jnp.concatenate([t[pl.ds(near, rows // 2), :], t[pl.ds(away, rows // 2), :]])
            for t in (cosine, sine)
        )
        for h in range(HEADS * GROUP):
            at = pl.multiple_of((core * HEADS * GROUP + h) * HD, HD)
            turned = turn(ref[:, pl.ds(at, HD)].astype(jnp.float32), cos, sin)
            rotated[h, pl.ds(first, rows), :] = (turned * scale).astype(jnp.bfloat16)


def merge_kernel(size, meta, own, other, merged):
    core = meta[0]
    rows = own.shape[1]
    for ref, place in ((own, core), (other, 1 - core)):
        for g in range(own.shape[0]):
            for n in range(rows // size):
                at = pl.multiple_of((n * CORES + place) * size, size)
                merged[g, pl.ds(at, size), :] = ref[g, n * size : (n + 1) * size, :]


def project_kernel(rope, sources, meta, cosine, sine, *refs):
    acts = refs[:sources]
    pieces = refs[sources:-sources]
    outs = refs[-sources:]

    def rows_of(ref):
        total = None
        for i, piece in enumerate(pieces):
            term = jnp.dot(ref[meta[3 + i]], piece[...], preferred_element_type=jnp.float32)
            total = term if total is None else total + term
        return total

    def ready(total, at):
        if rope:
            stretch = slice(at, at + total.shape[0])
            total = turn(total, cosine[stretch, :], sine[stretch, :])
        return total.astype(jnp.bfloat16)

    block = acts[0].shape[1]
    made = ready(rows_of(acts[0]), 0)
    if sources == 1:
        outs[0][...] = made
        return
    rows = block // CORES
    outs[0][...] = made[:rows]
    outs[1][:rows, :] = made[rows:]

    @pl.when(meta[1] > 0)
    def _():
        outs[1][rows:, :] = ready(rows_of(acts[1]), block)

    @pl.when(meta[1] == 0)
    def _():
        outs[1][rows:, :] = jnp.zeros((rows, outs[1].shape[1]), jnp.bfloat16)


def slice_kernel(meta, whole, out):
    out[...] = whole[...]


def cut(meta, weight, at, width):
    return pl.pallas_call(
        slice_kernel,
        out_shape=jax.ShapeDtypeStruct((weight.shape[0], width), weight.dtype),
        grid_spec=pltpu.PrefetchScalarGridSpec(
            num_scalar_prefetch=1,
            grid=(1,),
            in_specs=[
                pl.BlockSpec(
                    (weight.shape[0], width),
                    lambda i, meta: (0, meta[0] * (HEADS * HD // width) + at // width),
                )
            ],
            out_specs=pl.BlockSpec((weight.shape[0], width), lambda i, meta: (0, 0)),
        ),
        compiler_params=pltpu.CompilerParams(vmem_limit_bytes=4 * MIB),
    )(meta, weight)


def attend_kernel(window, first_head, stage, key_at, value_at, meta, rotated, *refs):
    outs = 2 if stage != "open" else 0
    carried = 2 if stage == "close" else 0
    total, mixture = refs[-2:]
    if outs:
        out_own, out_other = refs[-4:-2]
    chip, core, length = meta[1], meta[0], meta[2]
    heads, block = GROUP, rotated.shape[1]
    first = chip * block
    half = block // CORES
    quarter = half // 2
    if carried:
        total_in, mixture_in = refs[:2]
        total[...] = total_in[...]
        mixture[...] = mixture_in[...]
        refs = refs[2:]

    def stretch(step, part, masked):
        ref, row, _ = key_at[step, part]
        keys = refs[ref][row : row + half, :]
        value = []
        for ref, row, column, size in value_at[step, part]:
            value.append(refs[ref][row : row + half, column : column + size])
        value = value[0] if len(value) == 1 else jnp.concatenate(value, axis=-1)
        mask = None
        if masked:
            shape = (block, half)
            q = first + lax.broadcasted_iota(jnp.int32, shape, 0)
            r = lax.broadcasted_iota(jnp.int32, shape, 1)
            k = first - step * block + part * quarter + r + jnp.where(r >= quarter, half - quarter, 0)
            mask = (k <= q) & (k < length)
            if window is not None:
                mask = mask & (q - k < window)
        for h in range(heads):
            scores = lax.dot_general(
                rotated[first_head + h],
                keys,
                (((1,), (1,)), ((), ())),
                preferred_element_type=jnp.float32,
            )
            weights = jnp.exp2(jnp.tanh(scores) * (SOFTCAP * math.log2(math.e)))
            if masked:
                weights = jnp.where(mask, weights, 0.0)
            summed = jnp.sum(weights, axis=-1, keepdims=True)
            product = jnp.dot(weights.astype(jnp.bfloat16), value, preferred_element_type=jnp.float32)
            if (step, part) == (0, 0):
                total[h], mixture[h] = summed, product
            else:
                total[h] += summed
                mixture[h] += product

    def group(step, parts, masked):
        for part in parts:
            stretch(step, part, masked)

    for step in sorted({s for s, _ in key_at}):
        parts = [p for s, p in sorted(key_at) if s == step]
        if step == 0:
            group(0, parts, True)
            continue
        inside = first - step * block + block <= length
        if window is not None:
            inside = inside & ((step + 1) * block <= window)
        pl.when((chip >= step) & inside)(functools.partial(group, step, parts, False))
        pl.when((chip >= step) & jnp.logical_not(inside))(functools.partial(group, step, parts, True))

    if outs:
        for ref, place in ((out_own, core), (out_other, 1 - core)):
            at = pl.multiple_of(place * half, half)
            position = first + at + lax.broadcasted_iota(jnp.int32, (half, 1), 0)
            valid = position < length
            for h in range(heads):
                safe = jnp.where(valid, total[h, pl.ds(at, half), :], 1.0)
                result = mixture[h, pl.ds(at, half), :] / safe
                ref[:, h * HD : (h + 1) * HD] = jnp.where(valid, result, 0.0).astype(jnp.bfloat16)


def call(kernel, outs, operands, scratch=(), flops=0, transcendentals=0, limit=None, scalars=1):
    return pl.pallas_call(
        kernel,
        out_shape=outs,
        in_specs=[SMEM] * scalars + [VMEM] * (len(operands) - scalars),
        out_specs=jax.tree.map(lambda _: VMEM, outs),
        scratch_shapes=list(scratch),
        cost_estimate=pl.CostEstimate(
            flops=flops,
            transcendentals=transcendentals,
            bytes_accessed=sum(x.size * x.dtype.itemsize for x in operands),
        ),
        compiler_params=pltpu.CompilerParams(vmem_limit_bytes=limit),
    )(*operands)


def local(seq, fsdp, hidden, queries, norm_gain, key_weight, value_weight, lengths):
    bf16 = jnp.bfloat16
    f32 = jnp.float32
    _, rows, depth = hidden.shape
    chips = seq // CORES
    block = rows * CORES
    lead = rows // 2
    shard = lax.axis_index("seq")
    core, chip = shard % CORES, shard // CORES
    member = lax.axis_index("fsdp")
    relay = fsdp == 4

    swap = [(i, i ^ 1) for i in range(seq)]
    both = ("seq", "fsdp")

    def route(offsets):
        return [
            (i * fsdp + j, i * fsdp + (j ^ offsets[i % CORES]))
            for i in range(seq)
            for j in range(fsdp)
        ]

    def climb(step):
        return [(s, s + CORES) for s in range((step - 1) * CORES, seq - CORES)]

    if relay:
        groups = 4
        ids = [member, member ^ (1 + core), member ^ (2 - core), member ^ 3]
    else:
        groups = 1
        ids = [0]
    meta = jnp.stack([jnp.asarray(v, jnp.int32) for v in [core, chip, lengths[0]] + ids])

    pieces = []
    for i, (kind, at, width, _) in enumerate(CHUNKS):
        weight = key_weight if kind == KEY else value_weight
        if i == 0:
            own = lax.dynamic_slice_in_dim(weight, core * HEADS * HD + at, width, 1)
        else:
            own = cut(meta, weight, at, width)
        if relay:
            near = lax.ppermute(own, both, route((1, 2)))
            next_ = lax.ppermute(own, both, route((2, 1)))
            far = lax.ppermute(near, both, route((2, 1)))
            pieces.append((own, near, next_, far))
        else:
            pieces.append((lax.all_gather(own, "fsdp", axis=0, tiled=True),))

    normed, leading = call(
        norm_kernel,
        (
            jax.ShapeDtypeStruct((groups, rows, depth // groups), bf16),
            jax.ShapeDtypeStruct((groups, lead, depth // groups), bf16),
        ),
        (hidden[0], norm_gain[None, :]),
        flops=5 * rows * depth,
        limit=24 * MIB,
        scalars=0,
    )

    def merge(size, own, other):
        return call(
            functools.partial(merge_kernel, size),
            jax.ShapeDtypeStruct((own.shape[0], CORES * own.shape[1], own.shape[2]), bf16),
            (meta, own, other),
            flops=own.size,
            limit=16 * MIB,
        )

    acts = (merge(lead, normed, lax.ppermute(normed, "seq", swap)),)
    if any(shifted for *_, shifted in CHUNKS):
        risen = lax.ppermute(leading, "seq", climb(1))
        more = (merge(lead, risen, lax.ppermute(risen, "seq", swap)),)
    q_other = lax.ppermute(queries[0], "seq", swap)

    exponent = jnp.arange(HD // 2, dtype=f32) * (2.0 / HD)
    frequency = jnp.exp(-jnp.log(10000.0) * exponent)

    def tables(slots):
        angles = slots.astype(f32)[:, None] * frequency[None, :]
        return jnp.cos(angles), jnp.sin(angles)

    slots = chip * block + jnp.arange(block, dtype=jnp.int32)
    ordered = slots.reshape(CORES, 2, lead).swapaxes(0, 1).reshape(block)
    laid = tables(jnp.concatenate([ordered, ordered[:rows] - block]))

    rotated = call(
        rope_kernel,
        jax.ShapeDtypeStruct((HEADS * GROUP, block, HD), bf16),
        (meta, queries[0], q_other, *laid),
        flops=10 * block * HEADS * GROUP * HD,
        limit=12 * MIB,
    )

    climbed = []
    for i, (kind, at, width, shifted) in enumerate(CHUNKS):
        sources = acts + more if shifted else acts
        made = call(
            functools.partial(project_kernel, kind == KEY, len(sources)),
            [
                jax.ShapeDtypeStruct((n, width), bf16)
                for n in ((rows, block) if shifted else (block,))
            ],
            (meta, *laid, *sources, *pieces[i]),
            flops=2 * block * depth * width,
            limit=12 * MIB,
        )
        steps = [made]
        for step in range(1, chips):
            sent = made[-1] if step == 1 else steps[-1]
            if shifted and step == chips - 1:
                sent = sent[:rows]
            steps.append(lax.ppermute(sent, "seq", climb(step)))
        climbed.append(steps)

    def place(shifted, step, part):
        if not shifted:
            return (step, part * rows) if step else ((0, 0), part * rows)
        if step == 0:
            return (0, part), 0
        if part == 1:
            return step, 0
        return ((0, 1), rows) if step == 1 else (step - 1, rows)

    window = WINDOW if WINDOW < chips * block else None
    mine, theirs = [], []
    for j in range(HEADS):
        stretches = [(step, part) for step in range(chips) for part in range(2)]
        stages = [("whole", stretches)]
        if j in SPLIT:
            stages = [("open", stretches[:-1]), ("close", stretches[-1:])]
        state = ()
        for stage, todo in stages:
            arrays, numbers = [], {}

            def number(i, step):
                if (i, step) not in numbers:
                    numbers[i, step] = len(arrays)
                    arrays.append(climbed[i][0][step[1]] if isinstance(step, tuple) else climbed[i][step])
                return numbers[i, step]

            key_at, value_at = {}, {}
            for i, (kind, at, width, shifted) in enumerate(CHUNKS):
                lo, hi = max(at, j * HD), min(at + width, (j + 1) * HD)
                if lo >= hi:
                    continue
                for spot in todo:
                    step, row = place(shifted, *spot)
                    if kind == KEY:
                        key_at[spot] = (number(i, step), row, 0)
                    else:
                        value_at.setdefault(spot, []).append((lo, number(i, step), row, lo - at, hi - lo))
            value_at = {spot: tuple(v[1:] for v in sorted(parts)) for spot, parts in value_at.items()}
            scratch = (
                pltpu.VMEM((GROUP, block, 1), f32),
                pltpu.VMEM((GROUP, block, HD), f32),
            )
            carry = (
                jax.ShapeDtypeStruct((GROUP, block, 1), f32),
                jax.ShapeDtypeStruct((GROUP, block, HD), f32),
            )
            results = (jax.ShapeDtypeStruct((rows, GROUP * HD), bf16),) * 2
            state = call(
                functools.partial(attend_kernel, window, j * GROUP, stage, key_at, value_at),
                carry if stage == "open" else results,
                (meta, rotated, *state, *arrays),
                scratch=() if stage == "open" else scratch,
                flops=4 * GROUP * block * rows * len(todo) * HD,
                transcendentals=2 * GROUP * block * rows * len(todo),
                limit=16 * MIB,
            )
        mine.append(state[0])
        theirs.append(lax.ppermute(state[1], "seq", swap))
    low = [jnp.where(core == 0, a, b) for a, b in zip(mine, theirs)]
    high = [jnp.where(core == 0, b, a) for a, b in zip(mine, theirs)]
    return jnp.concatenate(low + high, axis=1)[None]


def solution(mesh):
    in_specs = (
        P("fsdp", "seq", None),
        P("fsdp", "seq", None),
        P(),
        P("fsdp", None),
        P("fsdp", None),
        P("fsdp"),
    )
    out_specs = P("fsdp", "seq", None)
    seq, fsdp = mesh.shape["seq"], mesh.shape["fsdp"]

    def body(*args):
        return local(seq, fsdp, *args)

    return jax.shard_map(body, mesh=mesh, in_specs=in_specs, out_specs=out_specs, check_vma=False)
```

```python
import functools
import math

import jax
import jax.numpy as jnp
from jax import lax
from jax.experimental import pallas as pl
from jax.experimental.pallas import tpu as pltpu
from jax.sharding import PartitionSpec as P


HQ = 8
HK = 4
HD = 256
WINDOW = 4096

EPSILON = 1e-06
SOFTCAP = 50.0
CORES = 2
HEADS = HK // CORES
GROUP = HQ // HK
MIB = 1 << 20


VMEM = pl.BlockSpec(memory_space=pltpu.VMEM)
SMEM = pl.BlockSpec(memory_space=pltpu.SMEM)
HBM = pl.BlockSpec(memory_space=pltpu.HBM)

KEY, VALUE = "key", "value"
HALF = HD // 2
CHUNKS = (
    (KEY, 0, HD, False),
    (VALUE, 0, HD, True),
    (KEY, HD, HD, True),
    (VALUE, HD, HD, True),
)
SPLIT = (1,)


def turn(x, cos, sin):
    a, b = x[:, : HD // 2], x[:, HD // 2 :]
    return jnp.concatenate([a * cos - b * sin, b * cos + a * sin], axis=-1)


def normalize(rows, gain):
    floats = rows.astype(jnp.float32)
    factor = lax.rsqrt(jnp.mean(floats * floats, axis=-1, keepdims=True) + EPSILON)
    return (floats * factor * gain).astype(jnp.bfloat16)


def norm_kernel(gain, hidden, normed, held, sems):
    groups, rows, depth = normed.shape
    parts = sems.shape[0]
    size = rows // parts
    copies = [
        pltpu.make_async_copy(hidden.at[n * size : (n + 1) * size, :], held.at[n], sems.at[n])
        for n in range(parts)
    ]
    for copy in copies:
        copy.start()
    for n, copy in enumerate(copies):
        copy.wait()
        result = normalize(held[n], gain[...])
        for g in range(groups):
            normed[g, n * size : (n + 1) * size, :] = result[:, g * depth : (g + 1) * depth]


def lead_kernel(meta, gain, own, other, merged):
    groups, rows, depth = merged.shape
    lead = rows // CORES

    @pl.when(meta[1] > 0)
    def _():
        for ref, place in ((own, meta[0]), (other, 1 - meta[0])):
            result = normalize(ref[...], gain[...])
            for g in range(groups):
                at = pl.multiple_of(place * lead, lead)
                merged[g, pl.ds(at, lead), :] = result[:, g * depth : (g + 1) * depth]


def rope_kernel(meta, q_own, q_other, cosine, sine, rotated):
    core = meta[0]
    rows = q_own.shape[0]
    scale = 1.0 / (math.sqrt(HD) * SOFTCAP)
    for ref, place in ((q_own, core), (q_other, 1 - core)):
        first = pl.multiple_of(place * rows, rows)
        near = pl.multiple_of(place * (rows // 2), rows // 2)
        away = pl.multiple_of(rows + place * (rows // 2), rows // 2)
        cos, sin = (
            jnp.concatenate([t[pl.ds(near, rows // 2), :], t[pl.ds(away, rows // 2), :]])
            for t in (cosine, sine)
        )
        for h in range(HEADS * GROUP):
            at = pl.multiple_of((core * HEADS * GROUP + h) * HD, HD)
            turned = turn(ref[:, pl.ds(at, HD)].astype(jnp.float32), cos, sin)
            rotated[h, pl.ds(first, rows), :] = (turned * scale).astype(jnp.bfloat16)


def merge_kernel(size, meta, own, other, merged):
    core = meta[0]
    rows = own.shape[1]
    for ref, place in ((own, core), (other, 1 - core)):
        for g in range(own.shape[0]):
            for n in range(rows // size):
                at = pl.multiple_of((n * CORES + place) * size, size)
                merged[g, pl.ds(at, size), :] = ref[g, n * size : (n + 1) * size, :]


def project_kernel(rope, sources, meta, cosine, sine, *refs):
    acts = refs[:sources]
    pieces = refs[sources:-sources]
    outs = refs[-sources:]

    def rows_of(ref):
        total = None
        for i, piece in enumerate(pieces):
            term = jnp.dot(ref[meta[3 + i]], piece[...], preferred_element_type=jnp.float32)
            total = term if total is None else total + term
        return total

    def ready(total, at):
        if rope:
            stretch = slice(at, at + total.shape[0])
            total = turn(total, cosine[stretch, :], sine[stretch, :])
        return total.astype(jnp.bfloat16)

    block = acts[0].shape[1]
    made = ready(rows_of(acts[0]), 0)
    if sources == 1:
        outs[0][...] = made
        return
    rows = block // CORES
    outs[0][...] = made[:rows]
    outs[1][:rows, :] = made[rows:]

    @pl.when(meta[1] > 0)
    def _():
        outs[1][rows:, :] = ready(rows_of(acts[1]), block)

    @pl.when(meta[1] == 0)
    def _():
        outs[1][rows:, :] = jnp.zeros((rows, outs[1].shape[1]), jnp.bfloat16)


def cut_kernel(at, meta, weight, out, sem):
    width = out.shape[1]
    first = pl.multiple_of(meta[0] * HEADS * HD + at, HALF)
    copy = pltpu.make_async_copy(weight.at[:, pl.ds(first, width)], out, sem)
    copy.start()
    copy.wait()


def cut(meta, weight, at, width):
    return pl.pallas_call(
        functools.partial(cut_kernel, at),
        out_shape=jax.ShapeDtypeStruct((weight.shape[0], width), weight.dtype),
        in_specs=[SMEM, HBM],
        out_specs=VMEM,
        scratch_shapes=[pltpu.SemaphoreType.DMA],
        compiler_params=pltpu.CompilerParams(vmem_limit_bytes=4 * MIB),
    )(meta, weight)


def attend_kernel(window, first_head, stage, key_at, value_at, meta, rotated, *refs):
    outs = 2 if stage != "open" else 0
    carried = 2 if stage == "close" else 0
    total, mixture = refs[-2:]
    if outs:
        out_own, out_other = refs[-4:-2]
    chip, core, length = meta[1], meta[0], meta[2]
    heads, block = GROUP, rotated.shape[1]
    first = chip * block
    half = block // CORES
    quarter = half // 2
    if carried:
        total_in, mixture_in = refs[:2]
        total[...] = total_in[...]
        mixture[...] = mixture_in[...]
        refs = refs[2:]

    def stretch(step, part, masked):
        ref, row, _ = key_at[step, part]
        keys = refs[ref][row : row + half, :]
        value = []
        for ref, row, column, size in value_at[step, part]:
            value.append(refs[ref][row : row + half, column : column + size])
        value = value[0] if len(value) == 1 else jnp.concatenate(value, axis=-1)
        mask = None
        if masked:
            shape = (block, half)
            q = first + lax.broadcasted_iota(jnp.int32, shape, 0)
            r = lax.broadcasted_iota(jnp.int32, shape, 1)
            k = first - step * block + part * quarter + r + jnp.where(r >= quarter, half - quarter, 0)
            mask = (k <= q) & (k < length)
            if window is not None:
                mask = mask & (q - k < window)
        for h in range(heads):
            scores = lax.dot_general(
                rotated[first_head + h],
                keys,
                (((1,), (1,)), ((), ())),
                preferred_element_type=jnp.float32,
            )
            weights = jnp.exp2(jnp.tanh(scores) * (SOFTCAP * math.log2(math.e)))
            if masked:
                weights = jnp.where(mask, weights, 0.0)
            summed = jnp.sum(weights, axis=-1, keepdims=True)
            product = jnp.dot(weights.astype(jnp.bfloat16), value, preferred_element_type=jnp.float32)
            if (step, part) == (0, 0):
                total[h], mixture[h] = summed, product
            else:
                total[h] += summed
                mixture[h] += product

    def group(step, parts, masked):
        for part in parts:
            stretch(step, part, masked)

    for step in sorted({s for s, _ in key_at}):
        parts = [p for s, p in sorted(key_at) if s == step]
        if step == 0:
            group(0, parts, True)
            continue
        inside = first - step * block + block <= length
        if window is not None:
            inside = inside & ((step + 1) * block <= window)
        pl.when((chip >= step) & inside)(functools.partial(group, step, parts, False))
        pl.when((chip >= step) & jnp.logical_not(inside))(functools.partial(group, step, parts, True))

    if outs:
        for ref, place in ((out_own, core), (out_other, 1 - core)):
            at = pl.multiple_of(place * half, half)
            position = first + at + lax.broadcasted_iota(jnp.int32, (half, 1), 0)
            valid = position < length
            for h in range(heads):
                safe = jnp.where(valid, total[h, pl.ds(at, half), :], 1.0)
                result = mixture[h, pl.ds(at, half), :] / safe
                ref[:, h * HD : (h + 1) * HD] = jnp.where(valid, result, 0.0).astype(jnp.bfloat16)


def call(kernel, outs, operands, scratch=(), flops=0, transcendentals=0, limit=None, scalars=1):
    return pl.pallas_call(
        kernel,
        out_shape=outs,
        in_specs=[SMEM] * scalars + [VMEM] * (len(operands) - scalars),
        out_specs=jax.tree.map(lambda _: VMEM, outs),
        scratch_shapes=list(scratch),
        cost_estimate=pl.CostEstimate(
            flops=flops,
            transcendentals=transcendentals,
            bytes_accessed=sum(x.size * x.dtype.itemsize for x in operands),
        ),
        compiler_params=pltpu.CompilerParams(vmem_limit_bytes=limit),
    )(*operands)


def local(seq, fsdp, hidden, queries, norm_gain, key_weight, value_weight, lengths):
    bf16 = jnp.bfloat16
    f32 = jnp.float32
    _, rows, depth = hidden.shape
    chips = seq // CORES
    block = rows * CORES
    lead = rows // 2
    shard = lax.axis_index("seq")
    core, chip = shard % CORES, shard // CORES
    member = lax.axis_index("fsdp")
    relay = fsdp == 4

    swap = [(i, i ^ 1) for i in range(seq)]
    both = ("seq", "fsdp")

    def route(offsets):
        return [
            (i * fsdp + j, i * fsdp + (j ^ offsets[i % CORES]))
            for i in range(seq)
            for j in range(fsdp)
        ]

    def climb(step):
        return [(s, s + CORES) for s in range((step - 1) * CORES, seq - CORES)]

    if relay:
        groups = 4
        ids = [member, member ^ (1 + core), member ^ (2 - core), member ^ 3]
    else:
        groups = 1
        ids = [0]
    meta = jnp.stack([jnp.asarray(v, jnp.int32) for v in [core, chip, lengths[0]] + ids])

    pieces = []
    for i, (kind, at, width, _) in enumerate(CHUNKS):
        weight = key_weight if kind == KEY else value_weight
        if i == 0:
            own = lax.dynamic_slice_in_dim(weight, core * HEADS * HD + at, width, 1)
        else:
            own = cut(meta, weight, at, width)
        if relay:
            near = lax.ppermute(own, both, route((1, 2)))
            next_ = lax.ppermute(own, both, route((2, 1)))
            far = lax.ppermute(near, both, route((2, 1)))
            pieces.append((own, near, next_, far))
        else:
            pieces.append((lax.all_gather(own, "fsdp", axis=0, tiled=True),))

    gain = norm_gain[None, :]
    parts = 4
    normed = pl.pallas_call(
        norm_kernel,
        out_shape=jax.ShapeDtypeStruct((groups, rows, depth // groups), bf16),
        in_specs=[VMEM, HBM],
        out_specs=VMEM,
        scratch_shapes=[
            pltpu.VMEM((parts, rows // parts, depth), bf16),
            pltpu.SemaphoreType.DMA((parts,)),
        ],
        cost_estimate=pl.CostEstimate(
            flops=5 * rows * depth, transcendentals=0, bytes_accessed=4 * rows * depth
        ),
        compiler_params=pltpu.CompilerParams(vmem_limit_bytes=16 * MIB),
    )(gain, hidden[0])
    other = lax.ppermute(normed, "seq", swap)
    merged = call(
        functools.partial(merge_kernel, lead),
        jax.ShapeDtypeStruct((groups, block, depth // groups), bf16),
        (meta, normed, other),
        flops=normed.size,
        limit=16 * MIB,
    )
    acts = (merged,)
    if any(shifted for *_, shifted in CHUNKS):
        risen = lax.ppermute(hidden[0, :lead], "seq", climb(1))
        across = lax.ppermute(risen, "seq", swap)
        more = call(
            lead_kernel,
            jax.ShapeDtypeStruct((groups, rows, depth // groups), bf16),
            (meta, gain, risen, across),
            flops=5 * rows * depth,
            limit=16 * MIB,
        )
        more = (more,)
    q_other = lax.ppermute(queries[0], "seq", swap)

    exponent = jnp.arange(HD // 2, dtype=f32) * (2.0 / HD)
    frequency = jnp.exp(-jnp.log(10000.0) * exponent)

    def tables(slots):
        angles = slots.astype(f32)[:, None] * frequency[None, :]
        return jnp.cos(angles), jnp.sin(angles)

    slots = chip * block + jnp.arange(block, dtype=jnp.int32)
    ordered = slots.reshape(CORES, 2, lead).swapaxes(0, 1).reshape(block)
    laid = tables(jnp.concatenate([ordered, ordered[:rows] - block]))

    rotated = call(
        rope_kernel,
        jax.ShapeDtypeStruct((HEADS * GROUP, block, HD), bf16),
        (meta, queries[0], q_other, *laid),
        flops=10 * block * HEADS * GROUP * HD,
        limit=12 * MIB,
    )

    climbed = []
    for i, (kind, at, width, shifted) in enumerate(CHUNKS):
        sources = acts + more if shifted else acts
        made = call(
            functools.partial(project_kernel, kind == KEY, len(sources)),
            [
                jax.ShapeDtypeStruct((n, width), bf16)
                for n in ((rows, block) if shifted else (block,))
            ],
            (meta, *laid, *sources, *pieces[i]),
            flops=2 * block * depth * width,
            limit=12 * MIB,
        )
        steps = [made]
        for step in range(1, chips):
            sent = made[-1] if step == 1 else steps[-1]
            if shifted and step == chips - 1:
                sent = sent[:rows]
            steps.append(lax.ppermute(sent, "seq", climb(step)))
        climbed.append(steps)

    def place(shifted, step, part):
        if not shifted:
            return (step, part * rows) if step else ((0, 0), part * rows)
        if step == 0:
            return (0, part), 0
        if part == 1:
            return step, 0
        return ((0, 1), rows) if step == 1 else (step - 1, rows)

    window = WINDOW if WINDOW < chips * block else None
    mine, theirs = [], []
    for j in range(HEADS):
        stretches = [(step, part) for step in range(chips) for part in range(2)]
        stages = [("whole", stretches)]
        if j in SPLIT:
            stages = [("open", stretches[:-1]), ("close", stretches[-1:])]
        state = ()
        for stage, todo in stages:
            arrays, numbers = [], {}

            def number(i, step):
                if (i, step) not in numbers:
                    numbers[i, step] = len(arrays)
                    arrays.append(climbed[i][0][step[1]] if isinstance(step, tuple) else climbed[i][step])
                return numbers[i, step]

            key_at, value_at = {}, {}
            for i, (kind, at, width, shifted) in enumerate(CHUNKS):
                lo, hi = max(at, j * HD), min(at + width, (j + 1) * HD)
                if lo >= hi:
                    continue
                for spot in todo:
                    step, row = place(shifted, *spot)
                    if kind == KEY:
                        key_at[spot] = (number(i, step), row, 0)
                    else:
                        value_at.setdefault(spot, []).append((lo, number(i, step), row, lo - at, hi - lo))
            value_at = {spot: tuple(v[1:] for v in sorted(parts)) for spot, parts in value_at.items()}
            scratch = (
                pltpu.VMEM((GROUP, block, 1), f32),
                pltpu.VMEM((GROUP, block, HD), f32),
            )
            carry = (
                jax.ShapeDtypeStruct((GROUP, block, 1), f32),
                jax.ShapeDtypeStruct((GROUP, block, HD), f32),
            )
            results = (jax.ShapeDtypeStruct((rows, GROUP * HD), bf16),) * 2
            state = call(
                functools.partial(attend_kernel, window, j * GROUP, stage, key_at, value_at),
                carry if stage == "open" else results,
                (meta, rotated, *state, *arrays),
                scratch=() if stage == "open" else scratch,
                flops=4 * GROUP * block * rows * len(todo) * HD,
                transcendentals=2 * GROUP * block * rows * len(todo),
                limit=16 * MIB,
            )
        mine.append(state[0])
        theirs.append(lax.ppermute(state[1], "seq", swap))
    low = [jnp.where(core == 0, a, b) for a, b in zip(mine, theirs)]
    high = [jnp.where(core == 0, b, a) for a, b in zip(mine, theirs)]
    return jnp.concatenate(low + high, axis=1)[None]


def solution(mesh):
    in_specs = (
        P("fsdp", "seq", None),
        P("fsdp", "seq", None),
        P(),
        P("fsdp", None),
        P("fsdp", None),
        P("fsdp"),
    )
    out_specs = P("fsdp", "seq", None)
    seq, fsdp = mesh.shape["seq"], mesh.shape["fsdp"]

    def body(*args):
        return local(seq, fsdp, *args)

    return jax.shard_map(body, mesh=mesh, in_specs=in_specs, out_specs=out_specs, check_vma=False)
```

```python
import functools
import math

import jax
import jax.numpy as jnp
from jax import lax
from jax.experimental import pallas as pl
from jax.experimental.pallas import tpu as pltpu
from jax.sharding import PartitionSpec as P


HQ = 8
HK = 4
HD = 256
WINDOW = 4096

EPSILON = 1e-06
SOFTCAP = 50.0
CORES = 2
HEADS = HK // CORES
GROUP = HQ // HK
MIB = 1 << 20


VMEM = pl.BlockSpec(memory_space=pltpu.VMEM)
SMEM = pl.BlockSpec(memory_space=pltpu.SMEM)
HBM = pl.BlockSpec(memory_space=pltpu.HBM)

KEY, VALUE = "key", "value"
HALF = HD // 2
CHUNKS = (
    (KEY, 0, HD, False),
    (VALUE, 0, HD, True),
    (KEY, HD, HD, True),
    (VALUE, HD, HD, True),
)
SPLIT = (1,)

LATE = (3,)


def turn(x, cos, sin):
    a, b = x[:, : HD // 2], x[:, HD // 2 :]
    return jnp.concatenate([a * cos - b * sin, b * cos + a * sin], axis=-1)


def normalize(rows, gain):
    floats = rows.astype(jnp.float32)
    factor = lax.rsqrt(jnp.mean(floats * floats, axis=-1, keepdims=True) + EPSILON)
    return (floats * factor * gain).astype(jnp.bfloat16)


def norm_kernel(gain, hidden, normed, held, sems):
    groups, rows, depth = normed.shape
    parts = sems.shape[0]
    size = rows // parts
    copies = [
        pltpu.make_async_copy(hidden.at[n * size : (n + 1) * size, :], held.at[n], sems.at[n])
        for n in range(parts)
    ]
    for copy in copies:
        copy.start()
    for n, copy in enumerate(copies):
        copy.wait()
        result = normalize(held[n], gain[...])
        for g in range(groups):
            normed[g, n * size : (n + 1) * size, :] = result[:, g * depth : (g + 1) * depth]


def lead_kernel(meta, gain, own, other, merged):
    groups, rows, depth = merged.shape
    lead = rows // CORES

    @pl.when(meta[1] > 0)
    def _():
        for ref, place in ((own, meta[0]), (other, 1 - meta[0])):
            result = normalize(ref[...], gain[...])
            for g in range(groups):
                at = pl.multiple_of(place * lead, lead)
                merged[g, pl.ds(at, lead), :] = result[:, g * depth : (g + 1) * depth]


def rope_kernel(meta, q_own, q_other, cosine, sine, rotated):
    core = meta[0]
    rows = q_own.shape[0]
    scale = 1.0 / (math.sqrt(HD) * SOFTCAP)
    for ref, place in ((q_own, core), (q_other, 1 - core)):
        first = pl.multiple_of(place * rows, rows)
        near = pl.multiple_of(place * (rows // 2), rows // 2)
        away = pl.multiple_of(rows + place * (rows // 2), rows // 2)
        cos, sin = (
            jnp.concatenate([t[pl.ds(near, rows // 2), :], t[pl.ds(away, rows // 2), :]])
            for t in (cosine, sine)
        )
        for h in range(HEADS * GROUP):
            at = pl.multiple_of((core * HEADS * GROUP + h) * HD, HD)
            turned = turn(ref[:, pl.ds(at, HD)].astype(jnp.float32), cos, sin)
            rotated[h, pl.ds(first, rows), :] = (turned * scale).astype(jnp.bfloat16)


def merge_kernel(size, meta, own, other, merged):
    core = meta[0]
    rows = own.shape[1]
    for ref, place in ((own, core), (other, 1 - core)):
        for g in range(own.shape[0]):
            for n in range(rows // size):
                at = pl.multiple_of((n * CORES + place) * size, size)
                merged[g, pl.ds(at, size), :] = ref[g, n * size : (n + 1) * size, :]


def project_kernel(rope, sources, numbers, stage, meta, cosine, sine, *refs):
    carried, outs = (), refs[-sources:]
    if stage == "close":
        carried, refs = refs[:sources], refs[sources:]
    acts = refs[:sources]
    pieces = refs[sources:-sources]

    def rows_of(n):
        total = carried[n][...] if carried else None
        for i, piece in zip(numbers, pieces):
            term = jnp.dot(acts[n][meta[3 + i]], piece[...], preferred_element_type=jnp.float32)
            total = term if total is None else total + term
        return total

    def ready(total, at):
        if rope:
            stretch = slice(at, at + total.shape[0])
            total = turn(total, cosine[stretch, :], sine[stretch, :])
        return total.astype(jnp.bfloat16)

    if stage == "open":
        for n in range(sources):
            outs[n][...] = rows_of(n)
        return
    block = acts[0].shape[1]
    made = ready(rows_of(0), 0)
    if sources == 1:
        outs[0][...] = made
        return
    rows = block // CORES
    outs[0][...] = made[:rows]
    outs[1][:rows, :] = made[rows:]

    @pl.when(meta[1] > 0)
    def _():
        outs[1][rows:, :] = ready(rows_of(1), block)

    @pl.when(meta[1] == 0)
    def _():
        outs[1][rows:, :] = jnp.zeros((rows, outs[1].shape[1]), jnp.bfloat16)


def cut_kernel(at, meta, weight, out, sem):
    first = pl.multiple_of(meta[0] * HEADS * HD + at, HALF)
    copy = pltpu.make_async_copy(weight.at[:, pl.ds(first, out.shape[1])], out, sem)
    copy.start()
    copy.wait()


def cut(meta, weight, at, width):
    return pl.pallas_call(
        functools.partial(cut_kernel, at),
        out_shape=jax.ShapeDtypeStruct((weight.shape[0], width), weight.dtype),
        in_specs=[SMEM, HBM],
        out_specs=VMEM,
        scratch_shapes=[pltpu.SemaphoreType.DMA],
        compiler_params=pltpu.CompilerParams(vmem_limit_bytes=4 * MIB),
    )(meta, weight)


def attend_kernel(window, first_head, stage, key_at, value_at, meta, rotated, *refs):
    outs = 2 if stage != "open" else 0
    carried = 2 if stage == "close" else 0
    total, mixture = refs[-2:]
    if outs:
        out_own, out_other = refs[-4:-2]
    chip, core, length = meta[1], meta[0], meta[2]
    heads, block = GROUP, rotated.shape[1]
    first = chip * block
    half = block // CORES
    quarter = half // 2
    if carried:
        total_in, mixture_in = refs[:2]
        total[...] = total_in[...]
        mixture[...] = mixture_in[...]
        refs = refs[2:]

    def stretch(step, part, masked):
        ref, row, _ = key_at[step, part]
        keys = refs[ref][row : row + half, :]
        value = []
        for ref, row, column, size in value_at[step, part]:
            value.append(refs[ref][row : row + half, column : column + size])
        value = value[0] if len(value) == 1 else jnp.concatenate(value, axis=-1)
        mask = None
        if masked:
            shape = (block, half)
            q = first + lax.broadcasted_iota(jnp.int32, shape, 0)
            r = lax.broadcasted_iota(jnp.int32, shape, 1)
            k = first - step * block + part * quarter + r + jnp.where(r >= quarter, half - quarter, 0)
            mask = (k <= q) & (k < length)
            if window is not None:
                mask = mask & (q - k < window)
        for h in range(heads):
            scores = lax.dot_general(
                rotated[first_head + h],
                keys,
                (((1,), (1,)), ((), ())),
                preferred_element_type=jnp.float32,
            )
            weights = jnp.exp2(jnp.tanh(scores) * (SOFTCAP * math.log2(math.e)))
            if masked:
                weights = jnp.where(mask, weights, 0.0)
            summed = jnp.sum(weights, axis=-1, keepdims=True)
            product = jnp.dot(weights.astype(jnp.bfloat16), value, preferred_element_type=jnp.float32)
            if (step, part) == (0, 0):
                total[h], mixture[h] = summed, product
            else:
                total[h] += summed
                mixture[h] += product

    def group(step, parts, masked):
        for part in parts:
            stretch(step, part, masked)

    for step in sorted({s for s, _ in key_at}):
        parts = [p for s, p in sorted(key_at) if s == step]
        if step == 0:
            group(0, parts, True)
            continue
        inside = first - step * block + block <= length
        if window is not None:
            inside = inside & ((step + 1) * block <= window)
        pl.when((chip >= step) & inside)(functools.partial(group, step, parts, False))
        pl.when((chip >= step) & jnp.logical_not(inside))(functools.partial(group, step, parts, True))

    if outs:
        for ref, place in ((out_own, core), (out_other, 1 - core)):
            at = pl.multiple_of(place * half, half)
            position = first + at + lax.broadcasted_iota(jnp.int32, (half, 1), 0)
            valid = position < length
            for h in range(heads):
                safe = jnp.where(valid, total[h, pl.ds(at, half), :], 1.0)
                result = mixture[h, pl.ds(at, half), :] / safe
                ref[:, h * HD : (h + 1) * HD] = jnp.where(valid, result, 0.0).astype(jnp.bfloat16)


def call(kernel, outs, operands, scratch=(), flops=0, transcendentals=0, limit=None, scalars=1):
    return pl.pallas_call(
        kernel,
        out_shape=outs,
        in_specs=[SMEM] * scalars + [VMEM] * (len(operands) - scalars),
        out_specs=jax.tree.map(lambda _: VMEM, outs),
        scratch_shapes=list(scratch),
        cost_estimate=pl.CostEstimate(
            flops=flops,
            transcendentals=transcendentals,
            bytes_accessed=sum(x.size * x.dtype.itemsize for x in operands),
        ),
        compiler_params=pltpu.CompilerParams(vmem_limit_bytes=limit),
    )(*operands)


def local(seq, fsdp, hidden, queries, norm_gain, key_weight, value_weight, lengths):
    bf16 = jnp.bfloat16
    f32 = jnp.float32
    _, rows, depth = hidden.shape
    chips = seq // CORES
    block = rows * CORES
    lead = rows // 2
    shard = lax.axis_index("seq")
    core, chip = shard % CORES, shard // CORES
    member = lax.axis_index("fsdp")
    relay = fsdp == 4

    swap = [(i, i ^ 1) for i in range(seq)]
    both = ("seq", "fsdp")

    def route(offsets):
        return [
            (i * fsdp + j, i * fsdp + (j ^ offsets[i % CORES]))
            for i in range(seq)
            for j in range(fsdp)
        ]

    def climb(step):
        return [(s, s + CORES) for s in range((step - 1) * CORES, seq - CORES)]

    if relay:
        groups = 4
        ids = [member, member ^ (1 + core), member ^ (2 - core), member ^ 3]
    else:
        groups = 1
        ids = [0]
    meta = jnp.stack([jnp.asarray(v, jnp.int32) for v in [core, chip, lengths[0]] + ids])

    pieces = []
    for i, (kind, at, width, _) in enumerate(CHUNKS):
        weight = key_weight if kind == KEY else value_weight
        if i == 0:
            own = lax.dynamic_slice_in_dim(weight, core * HEADS * HD + at, width, 1)
        else:
            own = cut(meta, weight, at, width)
        if relay:
            near = lax.ppermute(own, both, route((1, 2)))
            next_ = lax.ppermute(own, both, route((2, 1)))
            far = lax.ppermute(near, both, route((2, 1)))
            pieces.append((own, near, next_, far))
        else:
            pieces.append((lax.all_gather(own, "fsdp", axis=0, tiled=True),))

    gain = norm_gain[None, :]
    parts = 4
    normed = pl.pallas_call(
        norm_kernel,
        out_shape=jax.ShapeDtypeStruct((groups, rows, depth // groups), bf16),
        in_specs=[VMEM, HBM],
        out_specs=VMEM,
        scratch_shapes=[
            pltpu.VMEM((parts, rows // parts, depth), bf16),
            pltpu.SemaphoreType.DMA((parts,)),
        ],
        cost_estimate=pl.CostEstimate(
            flops=5 * rows * depth, transcendentals=0, bytes_accessed=4 * rows * depth
        ),
        compiler_params=pltpu.CompilerParams(vmem_limit_bytes=16 * MIB),
    )(gain, hidden[0])
    other = lax.ppermute(normed, "seq", swap)
    merged = call(
        functools.partial(merge_kernel, lead),
        jax.ShapeDtypeStruct((groups, block, depth // groups), bf16),
        (meta, normed, other),
        flops=normed.size,
        limit=16 * MIB,
    )
    acts = (merged,)
    if any(shifted for *_, shifted in CHUNKS):
        risen = lax.ppermute(hidden[0, :lead], "seq", climb(1))
        across = lax.ppermute(risen, "seq", swap)
        more = call(
            lead_kernel,
            jax.ShapeDtypeStruct((groups, rows, depth // groups), bf16),
            (meta, gain, risen, across),
            flops=5 * rows * depth,
            limit=16 * MIB,
        )
        more = (more,)
    q_other = lax.ppermute(queries[0], "seq", swap)

    exponent = jnp.arange(HD // 2, dtype=f32) * (2.0 / HD)
    frequency = jnp.exp(-jnp.log(10000.0) * exponent)

    def tables(slots):
        angles = slots.astype(f32)[:, None] * frequency[None, :]
        return jnp.cos(angles), jnp.sin(angles)

    slots = chip * block + jnp.arange(block, dtype=jnp.int32)
    ordered = slots.reshape(CORES, 2, lead).swapaxes(0, 1).reshape(block)
    laid = tables(jnp.concatenate([ordered, ordered[:rows] - block]))

    rotated = call(
        rope_kernel,
        jax.ShapeDtypeStruct((HEADS * GROUP, block, HD), bf16),
        (meta, queries[0], q_other, *laid),
        flops=10 * block * HEADS * GROUP * HD,
        limit=12 * MIB,
    )

    climbed = []
    for i, (kind, at, width, shifted) in enumerate(CHUNKS):
        sources = acts + more if shifted else acts
        results = [
            jax.ShapeDtypeStruct((n, width), bf16)
            for n in ((rows, block) if shifted else (block,))
        ]
        stages = [("whole", tuple(range(len(pieces[i]))))]
        if i in LATE and relay:
            stages = [("open", (0, 1, 3)), ("close", (2,))]
        made = ()
        for stage, numbers in stages:
            sums = [jax.ShapeDtypeStruct((x.shape[1], width), f32) for x in sources]
            made = call(
                functools.partial(project_kernel, kind == KEY, len(sources), numbers, stage),
                sums if stage == "open" else results,
                (meta, *laid, *made, *sources, *[pieces[i][n] for n in numbers]),
                flops=2 * block * depth * width * len(numbers) // len(pieces[i]),
                limit=12 * MIB,
            )
        steps = [made]
        for step in range(1, chips):
            sent = made[-1] if step == 1 else steps[-1]
            if shifted and step == chips - 1:
                sent = sent[:rows]
            steps.append(lax.ppermute(sent, "seq", climb(step)))
        climbed.append(steps)

    def place(shifted, step, part):
        if not shifted:
            return (step, part * rows) if step else ((0, 0), part * rows)
        if step == 0:
            return (0, part), 0
        if part == 1:
            return step, 0
        return ((0, 1), rows) if step == 1 else (step - 1, rows)

    window = WINDOW if WINDOW < chips * block else None
    mine, theirs = [], []
    for j in range(HEADS):
        stretches = [(step, part) for step in range(chips) for part in range(2)]
        stages = [("whole", stretches)]
        if j in SPLIT:
            stages = [("open", stretches[:-1]), ("close", stretches[-1:])]
        state = ()
        for stage, todo in stages:
            arrays, numbers = [], {}

            def number(i, step):
                if (i, step) not in numbers:
                    numbers[i, step] = len(arrays)
                    arrays.append(climbed[i][0][step[1]] if isinstance(step, tuple) else climbed[i][step])
                return numbers[i, step]

            key_at, value_at = {}, {}
            for i, (kind, at, width, shifted) in enumerate(CHUNKS):
                lo, hi = max(at, j * HD), min(at + width, (j + 1) * HD)
                if lo >= hi:
                    continue
                for spot in todo:
                    step, row = place(shifted, *spot)
                    if kind == KEY:
                        key_at[spot] = (number(i, step), row, 0)
                    else:
                        value_at.setdefault(spot, []).append((lo, number(i, step), row, lo - at, hi - lo))
            value_at = {spot: tuple(v[1:] for v in sorted(parts)) for spot, parts in value_at.items()}
            scratch = (
                pltpu.VMEM((GROUP, block, 1), f32),
                pltpu.VMEM((GROUP, block, HD), f32),
            )
            carry = (
                jax.ShapeDtypeStruct((GROUP, block, 1), f32),
                jax.ShapeDtypeStruct((GROUP, block, HD), f32),
            )
            results = (jax.ShapeDtypeStruct((rows, GROUP * HD), bf16),) * 2
            state = call(
                functools.partial(attend_kernel, window, j * GROUP, stage, key_at, value_at),
                carry if stage == "open" else results,
                (meta, rotated, *state, *arrays),
                scratch=() if stage == "open" else scratch,
                flops=4 * GROUP * block * rows * len(todo) * HD,
                transcendentals=2 * GROUP * block * rows * len(todo),
                limit=16 * MIB,
            )
        mine.append(state[0])
        theirs.append(lax.ppermute(state[1], "seq", swap))
    low = [jnp.where(core == 0, a, b) for a, b in zip(mine, theirs)]
    high = [jnp.where(core == 0, b, a) for a, b in zip(mine, theirs)]
    return jnp.concatenate(low + high, axis=1)[None]


def solution(mesh):
    in_specs = (
        P("fsdp", "seq", None),
        P("fsdp", "seq", None),
        P(),
        P("fsdp", None),
        P("fsdp", None),
        P("fsdp"),
    )
    out_specs = P("fsdp", "seq", None)
    seq, fsdp = mesh.shape["seq"], mesh.shape["fsdp"]

    def body(*args):
        return local(seq, fsdp, *args)

    return jax.shard_map(body, mesh=mesh, in_specs=in_specs, out_specs=out_specs, check_vma=False)
```

```python
import functools
import math

import jax
import jax.numpy as jnp
from jax import lax
from jax.experimental import pallas as pl
from jax.experimental.pallas import tpu as pltpu
from jax.sharding import PartitionSpec as P


HQ = 8
HK = 4
HD = 256
WINDOW = 4096

EPSILON = 1e-06
SOFTCAP = 50.0
CORES = 2
HEADS = HK // CORES
GROUP = HQ // HK
MIB = 1 << 20


VMEM = pl.BlockSpec(memory_space=pltpu.VMEM)
SMEM = pl.BlockSpec(memory_space=pltpu.SMEM)
HBM = pl.BlockSpec(memory_space=pltpu.HBM)

KEY, VALUE = "key", "value"
HALF = HD // 2
CHUNKS = (
    (KEY, 0, HD, False),
    (VALUE, 0, HD, True),
    (KEY, HD, HD, True),
    (VALUE, HD, HD, True),
)
SPLIT = (1,)

LATE = (3,)


def turn(x, cos, sin):
    a, b = x[:, : HD // 2], x[:, HD // 2 :]
    return jnp.concatenate([a * cos - b * sin, b * cos + a * sin], axis=-1)


def normalize(rows, gain):
    floats = rows.astype(jnp.float32)
    factor = lax.rsqrt(jnp.mean(floats * floats, axis=-1, keepdims=True) + EPSILON)
    return (floats * factor * gain).astype(jnp.bfloat16)


def norm_kernel(gain, hidden, normed, held, sems):
    groups, rows, depth = normed.shape
    parts = sems.shape[0]
    size = rows // parts
    copies = [
        pltpu.make_async_copy(hidden.at[n * size : (n + 1) * size, :], held.at[n], sems.at[n])
        for n in range(parts)
    ]
    for copy in copies:
        copy.start()
    for n, copy in enumerate(copies):
        copy.wait()
        result = normalize(held[n], gain[...])
        for g in range(groups):
            normed[g, n * size : (n + 1) * size, :] = result[:, g * depth : (g + 1) * depth]


def lead_kernel(meta, gain, own, other, merged):
    groups, rows, depth = merged.shape
    lead = rows // CORES

    @pl.when(meta[1] > 0)
    def _():
        for ref, place in ((own, meta[0]), (other, 1 - meta[0])):
            result = normalize(ref[...], gain[...])
            for g in range(groups):
                at = pl.multiple_of(place * lead, lead)
                merged[g, pl.ds(at, lead), :] = result[:, g * depth : (g + 1) * depth]


def rope_kernel(meta, q_own, q_other, cosine, sine, rotated):
    core = meta[0]
    rows = q_own.shape[0]
    scale = 1.0 / (math.sqrt(HD) * SOFTCAP)
    for ref, place in ((q_own, core), (q_other, 1 - core)):
        first = pl.multiple_of(place * rows, rows)
        near = pl.multiple_of(place * (rows // 2), rows // 2)
        away = pl.multiple_of(rows + place * (rows // 2), rows // 2)
        cos, sin = (
            jnp.concatenate([t[pl.ds(near, rows // 2), :], t[pl.ds(away, rows // 2), :]])
            for t in (cosine, sine)
        )
        for h in range(HEADS * GROUP):
            at = pl.multiple_of((core * HEADS * GROUP + h) * HD, HD)
            turned = turn(ref[:, pl.ds(at, HD)].astype(jnp.float32), cos, sin)
            rotated[h, pl.ds(first, rows), :] = (turned * scale).astype(jnp.bfloat16)


def merge_kernel(size, meta, own, other, merged):
    core = meta[0]
    rows = own.shape[1]
    for ref, place in ((own, core), (other, 1 - core)):
        for g in range(own.shape[0]):
            for n in range(rows // size):
                at = pl.multiple_of((n * CORES + place) * size, size)
                merged[g, pl.ds(at, size), :] = ref[g, n * size : (n + 1) * size, :]


def project_kernel(rope, sources, numbers, stage, meta, cosine, sine, *refs):
    carried, outs = (), refs[-sources:]
    if stage == "close":
        carried, refs = refs[:sources], refs[sources:]
    acts = refs[:sources]
    pieces = refs[sources:-sources]

    def rows_of(n):
        total = carried[n][...] if carried else None
        for i, piece in zip(numbers, pieces):
            term = jnp.dot(acts[n][meta[3 + i]], piece[...], preferred_element_type=jnp.float32)
            total = term if total is None else total + term
        return total

    def ready(total, at):
        if rope:
            stretch = slice(at, at + total.shape[0])
            total = turn(total, cosine[stretch, :], sine[stretch, :])
        return total.astype(jnp.bfloat16)

    if stage == "open":
        for n in range(sources):
            outs[n][...] = rows_of(n)
        return
    block = acts[0].shape[1]
    made = ready(rows_of(0), 0)
    if sources == 1:
        outs[0][...] = made
        return
    rows = block // CORES
    outs[0][...] = made[:rows]
    outs[1][:rows, :] = made[rows:]

    @pl.when(meta[1] > 0)
    def _():
        outs[1][rows:, :] = ready(rows_of(1), block)

    @pl.when(meta[1] == 0)
    def _():
        outs[1][rows:, :] = jnp.zeros((rows, outs[1].shape[1]), jnp.bfloat16)


def cut_kernel(at, meta, weight, out, sem):
    first = pl.multiple_of(meta[0] * HEADS * HD + at, HALF)
    copy = pltpu.make_async_copy(weight.at[:, pl.ds(first, out.shape[1])], out, sem)
    copy.start()
    copy.wait()


def cut(meta, weight, at, width):
    return pl.pallas_call(
        functools.partial(cut_kernel, at),
        out_shape=jax.ShapeDtypeStruct((weight.shape[0], width), weight.dtype),
        in_specs=[SMEM, HBM],
        out_specs=VMEM,
        scratch_shapes=[pltpu.SemaphoreType.DMA],
        compiler_params=pltpu.CompilerParams(vmem_limit_bytes=4 * MIB),
    )(meta, weight)


def attend_kernel(window, first_head, stage, key_at, value_at, meta, rotated, *refs):
    outs = 2 if stage != "open" else 0
    carried = 2 if stage == "close" else 0
    total, mixture = refs[-2:]
    if outs:
        out_own, out_other = refs[-4:-2]
    chip, core, length = meta[1], meta[0], meta[2]
    heads, block = GROUP, rotated.shape[1]
    first = chip * block
    half = block // CORES
    quarter = half // 2
    if carried:
        total_in, mixture_in = refs[:2]
        total[...] = total_in[...]
        mixture[...] = mixture_in[...]
        refs = refs[2:]

    def stretch(step, part, masked):
        ref, row, _ = key_at[step, part]
        keys = refs[ref][row : row + half, :]
        value = []
        for ref, row, column, size in value_at[step, part]:
            value.append(refs[ref][row : row + half, column : column + size])
        value = value[0] if len(value) == 1 else jnp.concatenate(value, axis=-1)
        mask = None
        if masked:
            shape = (block, half)
            q = first + lax.broadcasted_iota(jnp.int32, shape, 0)
            r = lax.broadcasted_iota(jnp.int32, shape, 1)
            k = first - step * block + part * quarter + r + jnp.where(r >= quarter, half - quarter, 0)
            mask = (k <= q) & (k < length)
            if window is not None:
                mask = mask & (q - k < window)
        for h in range(heads):
            scores = lax.dot_general(
                rotated[first_head + h],
                keys,
                (((1,), (1,)), ((), ())),
                preferred_element_type=jnp.float32,
            )
            weights = jnp.exp2(jnp.tanh(scores) * (SOFTCAP * math.log2(math.e)))
            if masked:
                weights = jnp.where(mask, weights, 0.0)
            summed = jnp.sum(weights, axis=-1, keepdims=True)
            product = jnp.dot(weights.astype(jnp.bfloat16), value, preferred_element_type=jnp.float32)
            if (step, part) == (0, 0):
                total[h], mixture[h] = summed, product
            else:
                total[h] += summed
                mixture[h] += product

    def group(step, parts, masked):
        for part in parts:
            stretch(step, part, masked)

    for step in sorted({s for s, _ in key_at}):
        parts = [p for s, p in sorted(key_at) if s == step]
        if step == 0:
            group(0, parts, True)
            continue
        inside = first - step * block + block <= length
        if window is not None:
            inside = inside & ((step + 1) * block <= window)
        pl.when((chip >= step) & inside)(functools.partial(group, step, parts, False))
        pl.when((chip >= step) & jnp.logical_not(inside))(functools.partial(group, step, parts, True))

    if outs:
        for ref, place in ((out_own, core), (out_other, 1 - core)):
            at = pl.multiple_of(place * half, half)
            position = first + at + lax.broadcasted_iota(jnp.int32, (half, 1), 0)
            valid = position < length
            for h in range(heads):
                safe = jnp.where(valid, total[h, pl.ds(at, half), :], 1.0)
                result = mixture[h, pl.ds(at, half), :] / safe
                ref[:, h * HD : (h + 1) * HD] = jnp.where(valid, result, 0.0).astype(jnp.bfloat16)


def join_kernel(meta, *refs):
    parts, out, sems = refs[:-2], refs[-2], refs[-1]
    wide = parts[0].shape[1]
    copies = []
    for n, part in enumerate(parts):
        place = meta[0] if n < HEADS else 1 - meta[0]
        at = pl.multiple_of((place * HEADS + n % HEADS) * wide, wide)
        copies.append(pltpu.make_async_copy(part, out.at[:, pl.ds(at, wide)], sems.at[n]))
    for copy in copies:
        copy.start()
    for copy in copies:
        copy.wait()


def call(kernel, outs, operands, scratch=(), flops=0, transcendentals=0, limit=None, scalars=1):
    return pl.pallas_call(
        kernel,
        out_shape=outs,
        in_specs=[SMEM] * scalars + [VMEM] * (len(operands) - scalars),
        out_specs=jax.tree.map(lambda _: VMEM, outs),
        scratch_shapes=list(scratch),
        cost_estimate=pl.CostEstimate(
            flops=flops,
            transcendentals=transcendentals,
            bytes_accessed=sum(x.size * x.dtype.itemsize for x in operands),
        ),
        compiler_params=pltpu.CompilerParams(vmem_limit_bytes=limit),
    )(*operands)


def local(seq, fsdp, hidden, queries, norm_gain, key_weight, value_weight, lengths):
    bf16 = jnp.bfloat16
    f32 = jnp.float32
    _, rows, depth = hidden.shape
    chips = seq // CORES
    block = rows * CORES
    lead = rows // 2
    shard = lax.axis_index("seq")
    core, chip = shard % CORES, shard // CORES
    member = lax.axis_index("fsdp")
    relay = fsdp == 4

    swap = [(i, i ^ 1) for i in range(seq)]
    both = ("seq", "fsdp")

    def route(offsets):
        return [
            (i * fsdp + j, i * fsdp + (j ^ offsets[i % CORES]))
            for i in range(seq)
            for j in range(fsdp)
        ]

    def climb(step):
        return [(s, s + CORES) for s in range((step - 1) * CORES, seq - CORES)]

    if relay:
        groups = 4
        ids = [member, member ^ (1 + core), member ^ (2 - core), member ^ 3]
    else:
        groups = 1
        ids = [0]
    meta = jnp.stack([jnp.asarray(v, jnp.int32) for v in [core, chip, lengths[0]] + ids])

    pieces = []
    for i, (kind, at, width, _) in enumerate(CHUNKS):
        weight = key_weight if kind == KEY else value_weight
        if i == 0:
            own = lax.dynamic_slice_in_dim(weight, core * HEADS * HD + at, width, 1)
        else:
            own = cut(meta, weight, at, width)
        if relay:
            near = lax.ppermute(own, both, route((1, 2)))
            next_ = lax.ppermute(own, both, route((2, 1)))
            far = lax.ppermute(near, both, route((2, 1)))
            pieces.append((own, near, next_, far))
        else:
            pieces.append((lax.all_gather(own, "fsdp", axis=0, tiled=True),))

    gain = norm_gain[None, :]
    parts = 4
    normed = pl.pallas_call(
        norm_kernel,
        out_shape=jax.ShapeDtypeStruct((groups, rows, depth // groups), bf16),
        in_specs=[VMEM, HBM],
        out_specs=VMEM,
        scratch_shapes=[
            pltpu.VMEM((parts, rows // parts, depth), bf16),
            pltpu.SemaphoreType.DMA((parts,)),
        ],
        cost_estimate=pl.CostEstimate(
            flops=5 * rows * depth, transcendentals=0, bytes_accessed=4 * rows * depth
        ),
        compiler_params=pltpu.CompilerParams(vmem_limit_bytes=16 * MIB),
    )(gain, hidden[0])
    other = lax.ppermute(normed, "seq", swap)
    merged = call(
        functools.partial(merge_kernel, lead),
        jax.ShapeDtypeStruct((groups, block, depth // groups), bf16),
        (meta, normed, other),
        flops=normed.size,
        limit=16 * MIB,
    )
    acts = (merged,)
    if any(shifted for *_, shifted in CHUNKS):
        risen = lax.ppermute(hidden[0, :lead], "seq", climb(1))
        across = lax.ppermute(risen, "seq", swap)
        more = call(
            lead_kernel,
            jax.ShapeDtypeStruct((groups, rows, depth // groups), bf16),
            (meta, gain, risen, across),
            flops=5 * rows * depth,
            limit=16 * MIB,
        )
        more = (more,)
    q_other = lax.ppermute(queries[0], "seq", swap)

    exponent = jnp.arange(HD // 2, dtype=f32) * (2.0 / HD)
    frequency = jnp.exp(-jnp.log(10000.0) * exponent)

    def tables(slots):
        angles = slots.astype(f32)[:, None] * frequency[None, :]
        return jnp.cos(angles), jnp.sin(angles)

    slots = chip * block + jnp.arange(block, dtype=jnp.int32)
    ordered = slots.reshape(CORES, 2, lead).swapaxes(0, 1).reshape(block)
    laid = tables(jnp.concatenate([ordered, ordered[:rows] - block]))

    rotated = call(
        rope_kernel,
        jax.ShapeDtypeStruct((HEADS * GROUP, block, HD), bf16),
        (meta, queries[0], q_other, *laid),
        flops=10 * block * HEADS * GROUP * HD,
        limit=12 * MIB,
    )

    climbed = []
    for i, (kind, at, width, shifted) in enumerate(CHUNKS):
        sources = acts + more if shifted else acts
        results = [
            jax.ShapeDtypeStruct((n, width), bf16)
            for n in ((rows, block) if shifted else (block,))
        ]
        stages = [("whole", tuple(range(len(pieces[i]))))]
        if i in LATE and relay:
            stages = [("open", (0, 1, 3)), ("close", (2,))]
        made = ()
        for stage, numbers in stages:
            sums = [jax.ShapeDtypeStruct((x.shape[1], width), f32) for x in sources]
            made = call(
                functools.partial(project_kernel, kind == KEY, len(sources), numbers, stage),
                sums if stage == "open" else results,
                (meta, *laid, *made, *sources, *[pieces[i][n] for n in numbers]),
                flops=2 * block * depth * width * len(numbers) // len(pieces[i]),
                limit=12 * MIB,
            )
        steps = [made]
        for step in range(1, chips):
            sent = made[-1] if step == 1 else steps[-1]
            if shifted and step == chips - 1:
                sent = sent[:rows]
            steps.append(lax.ppermute(sent, "seq", climb(step)))
        climbed.append(steps)

    def place(shifted, step, part):
        if not shifted:
            return (step, part * rows) if step else ((0, 0), part * rows)
        if step == 0:
            return (0, part), 0
        if part == 1:
            return step, 0
        return ((0, 1), rows) if step == 1 else (step - 1, rows)

    window = WINDOW if WINDOW < chips * block else None
    mine, theirs = [], []
    for j in range(HEADS):
        stretches = [(step, part) for step in range(chips) for part in range(2)]
        stages = [("whole", stretches)]
        if j in SPLIT:
            stages = [("open", stretches[:-1]), ("close", stretches[-1:])]
        state = ()
        for stage, todo in stages:
            arrays, numbers = [], {}

            def number(i, step):
                if (i, step) not in numbers:
                    numbers[i, step] = len(arrays)
                    arrays.append(climbed[i][0][step[1]] if isinstance(step, tuple) else climbed[i][step])
                return numbers[i, step]

            key_at, value_at = {}, {}
            for i, (kind, at, width, shifted) in enumerate(CHUNKS):
                lo, hi = max(at, j * HD), min(at + width, (j + 1) * HD)
                if lo >= hi:
                    continue
                for spot in todo:
                    step, row = place(shifted, *spot)
                    if kind == KEY:
                        key_at[spot] = (number(i, step), row, 0)
                    else:
                        value_at.setdefault(spot, []).append((lo, number(i, step), row, lo - at, hi - lo))
            value_at = {spot: tuple(v[1:] for v in sorted(parts)) for spot, parts in value_at.items()}
            scratch = (
                pltpu.VMEM((GROUP, block, 1), f32),
                pltpu.VMEM((GROUP, block, HD), f32),
            )
            carry = (
                jax.ShapeDtypeStruct((GROUP, block, 1), f32),
                jax.ShapeDtypeStruct((GROUP, block, HD), f32),
            )
            results = (jax.ShapeDtypeStruct((rows, GROUP * HD), bf16),) * 2
            state = call(
                functools.partial(attend_kernel, window, j * GROUP, stage, key_at, value_at),
                carry if stage == "open" else results,
                (meta, rotated, *state, *arrays),
                scratch=() if stage == "open" else scratch,
                flops=4 * GROUP * block * rows * len(todo) * HD,
                transcendentals=2 * GROUP * block * rows * len(todo),
                limit=16 * MIB,
            )
        mine.append(state[0])
        theirs.append(lax.ppermute(state[1], "seq", swap))
    parts = (*mine, *theirs)
    joined = pl.pallas_call(
        join_kernel,
        out_shape=jax.ShapeDtypeStruct((rows, HQ * HD), bf16),
        in_specs=[SMEM] + [VMEM] * len(parts),
        out_specs=HBM,
        scratch_shapes=[pltpu.SemaphoreType.DMA((len(parts),))],
        compiler_params=pltpu.CompilerParams(vmem_limit_bytes=8 * MIB),
    )(meta, *parts)
    return joined[None]


def solution(mesh):
    in_specs = (
        P("fsdp", "seq", None),
        P("fsdp", "seq", None),
        P(),
        P("fsdp", None),
        P("fsdp", None),
        P("fsdp"),
    )
    out_specs = P("fsdp", "seq", None)
    seq, fsdp = mesh.shape["seq"], mesh.shape["fsdp"]

    def body(*args):
        return local(seq, fsdp, *args)

    return jax.shard_map(body, mesh=mesh, in_specs=in_specs, out_specs=out_specs, check_vma=False)
```
